32 devices in a mesh: gx: 4 (over y, x), gy: 8 (over z, core).
Axes of the slice: x: 2, y: 2, z: 4, core: 2. Of those that a mesh axis runs over, the one named last changes fastest.
Arguments:
- velocity: float32 [3, 32, 128, 256], P(None, 'gx', 'gy'), may hold values from -6 to 6
- pressure: float32 [32, 128, 256], P('gx', 'gy'), may hold values from -4 to 4
- part_cell: int32 [4, 8, 8, 512], P('gx', 'gy'), may hold values from 0 to 32767
- part_count: int32 [4, 8, 8], P('gx', 'gy'), may hold values from 1 to 512, as said below
- grain_velocities: float32 [4, 8, 8, 3, 512], P('gx', 'gy'), may hold values from -6 to 6
- part_vol: float32 [4, 8, 8, 512], P('gx', 'gy'), may hold values from 0.05 to 0.3
Outputs:
- velocity_out: float32 [3, 32, 128, 256], P(None, 'gx', 'gy')
- pressure_out: float32 [32, 128, 256], P('gx', 'gy')
- drag: float32 [4, 8, 8, 3, 512], P('gx', 'gy')
The draws below stay inside these ranges and needn't reach their ends.
Inputs may be any that keep to these rules, and one draw needn't show every extreme that they name: Every DEM owner (a, b) has at least one c with part_count[a, b, c] equal to 512.
All inputs are finite; a program needn't handle non-finite values.
Results may differ from the reference program's by a relative error of at most 0.00002.
Values sent between devices are 32-bit elements; how exact they have to be, the bound alone decides.
A program may use at most 128 MiB of HBM per device.

```python
import jax
import jax.numpy as jnp

CX = 8
CY = 16
NZ = 256
SLOT_CAPACITY = 512
STEPS = 2
SWEEPS = 4
NX = 32
NY = 128
CELLS = 32768
N_GX = 4
N_GY = 8


def draw_part_count(key, part):
    first, second = jax.random.split(key)
    base = jax.random.randint(first, (N_GX, N_GY, N_GY), 1, SLOT_CAPACITY + 1)
    chosen = jax.random.randint(second, (N_GX, N_GY, 1), 0, N_GY)
    hit = jnp.arange(N_GY, dtype=jnp.int32)[None, None, :] == chosen
    return jnp.where(hit, SLOT_CAPACITY, base).astype(jnp.int32)


def set_ends(array, stream_key, low, largest):
    place = [jax.random.randint(jax.random.fold_in(stream_key, axis), (), 0, length) for axis, length in enumerate(array.shape)]
    longest = array.shape.index(max(array.shape))
    beside = place[:longest] + [(place[longest] + 1) % array.shape[longest]] + place[longest + 1:]
    return array.at[tuple(place)].set(low).at[tuple(beside)].set(largest)


def levels(key, extent, shards, least, high):
    factor_of = 1.0
    for dim, shards_of in shards:
        steps = jax.random.uniform(jax.random.fold_in(jax.random.fold_in(key, 6), dim), (shards_of,), jnp.float32, least / len(shards), high / len(shards))
        factor_of = factor_of * jnp.repeat(jnp.exp(steps), extent[dim] // shards_of).reshape((-1,) + (1,) * (len(extent) - 1 - dim))
    return factor_of


def scatter_about(rng, extent, deviation, bound, pieces=(), kind=jnp.bfloat16):
    level = levels(rng, extent, pieces, -0.22, 0.18) if pieces else 1.0
    result = jax.random.normal(rng, extent, jnp.float32) * deviation * level
    return jnp.minimum(jnp.maximum(result, -bound), bound).astype(kind)


def setup_inputs(seed: int = 0) -> dict:
    key_of = jax.random.split(jax.random.key(seed), 7)
    velocity = scatter_about(key_of[0], (3, NX, NY, NZ), 1.0, 6.0, ((1, 4), (2, 8)), jnp.float32)
    pressure = scatter_about(key_of[1], (NX, NY, NZ), 0.5, 4.0, ((0, 4), (1, 8)), jnp.float32)
    part_cell = set_ends(jax.random.randint(key_of[2], (N_GX, N_GY, N_GY, SLOT_CAPACITY), 0, CELLS), jax.random.fold_in(key_of[2], 1), 0, CELLS - 1).astype(jnp.int32)
    part_count = draw_part_count(jax.random.fold_in(key_of[6], 71), 0)
    grain_velocities = scatter_about(key_of[4], (N_GX, N_GY, N_GY, 3, SLOT_CAPACITY), 1.0, 6.0, ((0, 4), (1, 8)), jnp.float32)
    part_vol = jnp.clip(0.05 + 0.25 * jax.random.uniform(key_of[5], (N_GX, N_GY, N_GY, SLOT_CAPACITY), jnp.float32) ** levels(key_of[5], (N_GX, N_GY, N_GY, SLOT_CAPACITY), ((0, 4), (1, 8)), -0.2, 0.2), 0.05, 0.3)
    return {"velocity": velocity, "pressure": pressure, "part_cell": part_cell, "part_count": part_count, "grain_velocities": grain_velocities, "part_vol": part_vol}


drag_coefficient = 2.0
time_step = 0.25
viscosity = 0.2
eps_floor = 0.4


def cell_faces(padded):
    return [padded[..., 2:, 1:-1, 1:-1], padded[..., :-2, 1:-1, 1:-1],
            padded[..., 1:-1, 2:, 1:-1], padded[..., 1:-1, :-2, 1:-1],
            padded[..., 1:-1, 1:-1, 2:], padded[..., 1:-1, 1:-1, :-2]]


def padded_mesh_cells(field):
    widths = [(0, 0)] * (field.ndim - 3) + [(1, 1), (1, 1), (1, 1)]
    return jnp.pad(field, widths)


def laplacian_operator(padded_velocity_field, flow_velocity, padded_voidage, porous_medium):
    near = cell_faces(padded_velocity_field)
    kernel_weights = cell_faces(padded_voidage)
    total = jnp.zeros_like(flow_velocity)
    for index in range(6):
        total = total + 0.5 * (porous_medium + kernel_weights[index]) * (near[index] - flow_velocity) / porous_medium
    return total


def divergence(flux_pad):
    near = cell_faces(flux_pad)
    return (0.5 / time_step) * (((near[0][0] - near[1][0]) + (near[2][1] - near[3][1])) + (near[4][2] - near[5][2]))


def relaxation_terms(padded_pressure_field, padded_voidage):
    central_value = padded_voidage[1:-1, 1:-1, 1:-1]
    near = cell_faces(padded_pressure_field)
    kernel_weights = cell_faces(padded_voidage)
    numerator = jnp.zeros_like(central_value)
    denominator = jnp.zeros_like(central_value)
    for index in range(6):
        weight = 0.5 * (central_value + kernel_weights[index])
        numerator = numerator + weight * near[index]
        denominator = denominator + weight
    return numerator, denominator


def gradient(padded_pressure_field):
    near = cell_faces(padded_pressure_field)
    return jnp.stack([0.5 * (near[0] - near[1]), 0.5 * (near[2] - near[3]), 0.5 * (near[4] - near[5])])


def to_grid(flat):
    return flat.reshape(N_GX, N_GY, CX, CY, NZ).transpose(0, 2, 1, 3, 4).reshape(NX, NY, NZ)


def to_grid3(flat):
    return flat.reshape(N_GX, N_GY, CX, CY, NZ, 3).transpose(5, 0, 2, 1, 3, 4).reshape(3, NX, NY, NZ)


def gather_from_mesh(grid):
    return grid.reshape(N_GX, CX, N_GY, CY, NZ).transpose(0, 2, 1, 3, 4).reshape(-1)


def from_grid3(grid):
    return grid.reshape(3, N_GX, CX, N_GY, CY, NZ).transpose(0, 1, 3, 2, 4, 5).reshape(3, -1)


def reference(velocity, pressure, part_cell, part_count, grain_velocities, part_vol):
    slots = jnp.arange(SLOT_CAPACITY, dtype=jnp.int32)
    alive = slots[None, None, None, :] < part_count[..., None]
    grain_volume = jnp.where(alive, part_vol, jnp.float32(0.0))
    owner = (jnp.arange(N_GX, dtype=jnp.int32)[:, None, None, None] * N_GY
             + jnp.arange(N_GY, dtype=jnp.int32)[None, None, :, None])
    target_field = (owner * CELLS + part_cell).astype(jnp.int32).reshape(-1)
    total = N_GX * N_GY * CELLS
    solid_flat = jax.ops.segment_sum(grain_volume.reshape(-1), target_field, num_segments=total)
    carried = jnp.moveaxis(grain_volume[..., None, :] * grain_velocities, 3, 4).reshape(-1, 3)
    flux_flat = jax.ops.segment_sum(carried, target_field, num_segments=total)
    solid = to_grid(solid_flat)
    mass_flux = to_grid3(flux_flat)
    porous_medium = jnp.maximum(1.0 - solid, eps_floor)
    padded_voidage = padded_mesh_cells(porous_medium)
    for step in range(STEPS):
        spread_to_mesh = laplacian_operator(padded_mesh_cells(velocity), velocity, padded_voidage, porous_medium)
        force = drag_coefficient * (mass_flux - solid * velocity) / porous_medium
        guess = velocity + time_step * (viscosity * spread_to_mesh + force)
        source = divergence(padded_mesh_cells(porous_medium * guess))
        for sweep in range(SWEEPS):
            numerator, denominator = relaxation_terms(padded_mesh_cells(pressure), padded_voidage)
            pressure = (numerator - source) / denominator
        velocity = guess - time_step * gradient(padded_mesh_cells(pressure))
    flat_vel = from_grid3(velocity)
    flattened_voids = gather_from_mesh(porous_medium)
    cell_flow_speed = jnp.moveaxis(flat_vel[:, target_field].reshape(3, N_GX, N_GY, N_GY, SLOT_CAPACITY), 0, 3)
    cell_void_fraction = flattened_voids[target_field].reshape(N_GX, N_GY, N_GY, SLOT_CAPACITY)
    drag = (grain_volume[..., None, :] * drag_coefficient) * (cell_flow_speed - grain_velocities) / cell_void_fraction[..., None, :]
    return velocity, pressure, drag
```

```python
import jax
import jax.numpy as jnp
from jax import lax
from jax.experimental import pallas as pl
from jax.experimental.pallas import tpu as pltpu
from jax.sharding import PartitionSpec as P

STEPS = 2
SWEEPS = 4
DRAG = 2.0
DT = 0.25
VISC = 0.2
FLOOR = 0.4

WX = SWEEPS + 1
WY = 8
ROWS = 8

MESH = pl.DeviceIdType.MESH
F32 = jnp.float32
BF16 = jnp.bfloat16


def split(value):
    high = value.astype(BF16).astype(F32)
    return high, value - high


def body(n_gx, n_gy, count_ref, vel_ref, p_ref, cell_ref, gv_ref, vol_ref,
         vel_out, p_out, drag_out,
         v1, v2, pin1, pin2, pa, pb, src1, src2, sp, solid, mf, eps, coef, rate, pull,
         guess, flux, dep, pk, rk, dk, rd, ft, field_send, field_recv, part_send, part_recv):
    bx, by, nz = p_ref.shape
    ex, ey = bx + 2 * WX, by + 2 * WY
    slots = vol_ref.shape[-1]
    columns = bx * by
    ix, iy = lax.axis_index("gx"), lax.axis_index("gy")
    has = {("x", 0): ix > 0, ("x", 1): ix < n_gx - 1, ("y", 0): iy > 0, ("y", 1): iy < n_gy - 1}
    peer = {("x", 0): (ix - 1, iy), ("x", 1): (ix + 1, iy), ("y", 0): (ix, iy - 1), ("y", 1): (ix, iy + 1)}
    own_x, own_y = pl.ds(WX, bx), pl.ds(WY, by)

    barrier = pltpu.get_barrier_semaphore()
    for k in range(1, n_gy):
        pl.semaphore_signal(barrier, inc=1, device_id=(ix, lax.rem(iy + k, n_gy)), device_id_type=MESH)
    for side in (0, 1):
        @pl.when(has["x", side])
        def _():
            pl.semaphore_signal(barrier, inc=1, device_id=peer["x", side], device_id_type=MESH)

    slot = lax.broadcasted_iota(jnp.int32, (1, slots), 1)
    for c in range(n_gy):
        cell = cell_ref[pl.ds(c, 1), :]
        column = lax.div(cell, nz)
        pk[c, 0:1, :] = column.astype(F32)
        pk[c, 1:2, :] = (cell - column * nz).astype(F32)
        pk[c, 2:3, :] = jnp.where(slot < count_ref[c], vol_ref[pl.ds(c, 1), :], 0.0)
        pk[c, 3:6, :] = gv_ref[c]
        pk[c, 6:8, :] = jnp.zeros((2, slots), F32)

    fields = [v1.at[d] for d in range(3)] + [v2.at[d] for d in range(3)] + [mf.at[d] for d in range(3)]
    fields += [pin1, pin2, src1, src2, solid]
    for side in (0, 1):
        @pl.when(jnp.logical_not(has["x", side]))
        def _():
            for field in fields:
                at = 0 if side == 0 else WX + bx
                field[pl.ds(at, WX), own_y, :] = jnp.zeros((WX, by, nz), F32)

        @pl.when(jnp.logical_not(has["y", side]))
        def _():
            for field in fields:
                at = 0 if side == 0 else WY + by
                field[:, pl.ds(at, WY), :] = jnp.zeros((ex, WY, nz), F32)

    pl.semaphore_wait(barrier, n_gy - 1 + jnp.where(ix > 0, 1, 0) + jnp.where(ix < n_gx - 1, 1, 0))

    def particles(k, source, landing, bank):
        return pltpu.make_async_remote_copy(
            src_ref=source, dst_ref=landing, send_sem=part_send.at[bank, k], recv_sem=part_recv.at[bank, k],
            device_id=(ix, lax.rem(iy + k, n_gy)), device_id_type=MESH)

    def outgoing(k):
        return particles(k, pk.at[lax.rem(iy + k, n_gy)], rk.at[iy], 0)

    def incoming(k):
        return particles(k, pk.at[0], rk.at[lax.rem(iy + n_gy - k, n_gy)], 0)

    for k in range(1, n_gy):
        outgoing(k).start()
    rk[iy] = pk[iy]

    class Halo:
        def __init__(self, slot, ref, width, own=None, corners=True):
            self.slot, self.ref, self.width, self.own, self.corners = slot, ref, width, own, corners

        def copy(self, index, source, landing, to):
            return pltpu.make_async_remote_copy(
                src_ref=source, dst_ref=landing, send_sem=field_send.at[self.slot, index],
                recv_sem=field_recv.at[self.slot, index], device_id=to, device_id_type=MESH)

        def x_copy(self, side):
            w = self.width
            at = 0 if side == 0 else bx - w
            if self.own is None:
                source = self.ref.at[pl.ds(WX + at, w), own_y]
            else:
                source = self.own.at[pl.ds(at, w)]
            landing = self.ref.at[pl.ds(WX + bx if side == 0 else WX - w, w), own_y]
            return self.copy(side, source, landing, peer["x", side])

        def y_copy(self, side):
            at = 0 if side == 0 else by - WY
            if self.own is None:
                source = self.ref.at[own_x, pl.ds(WY + at, WY)]
            else:
                source = self.own.at[:, pl.ds(at, WY)]
            landing = self.ref.at[own_x, pl.ds(WY + by if side == 0 else 0, WY)]
            return self.copy(2 + side, source, landing, peer["y", side])

        def c_copy(self, side, end):
            w = self.width
            rows = pl.ds(WX - w if end == 0 else WX + bx, w)
            source = self.ref.at[rows, pl.ds(WY if side == 0 else by, WY)]
            landing = self.ref.at[rows, pl.ds(WY + by if side == 0 else 0, WY)]
            return self.copy(4 + 2 * side + end, source, landing, peer["y", side])

        def each(self, axis, act, flip=False):
            for side in (0, 1):
                @pl.when(has[axis, 1 - side if flip else side])
                def _():
                    if axis == "x":
                        act(self.x_copy(side))
                    else:
                        act(self.y_copy(side))

        def each_corner(self, act, flip=False):
            for side in (0, 1):
                @pl.when(has["y", 1 - side if flip else side])
                def _():
                    for end in (0, 1):
                        act(self.c_copy(side, end))

    sent = []

    def start(halos):
        for h in halos:
            h.each("x", lambda c: c.start())
        for h in halos:
            h.each("y", lambda c: c.start())
        sent.extend(halos)

    def relay(halos):
        for h in halos:
            h.each("x", lambda c: c.wait_recv(), flip=True)
            if h.corners:
                h.each_corner(lambda c: c.start())

    def arrive(halos):
        for h in halos:
            h.each("y", lambda c: c.wait_recv(), flip=True)
            if h.corners:
                h.each_corner(lambda c: c.wait_recv(), flip=True)

    h_vel = [[Halo(0, v1.at[0], 2, vel_ref.at[0]), Halo(1, v1.at[1], 1, vel_ref.at[1]), Halo(2, v1.at[2], 1, vel_ref.at[2], False)],
             [Halo(3, v2.at[0], 2), Halo(4, v2.at[1], 1), Halo(5, v2.at[2], 1, None, False)]]
    h_p = [[Halo(6, pin1, WX, p_ref)], [Halo(7, pin2, WX)]]
    h_src = [[Halo(8, src1, SWEEPS)], [Halo(9, src2, SWEEPS)]]
    h_solid = [Halo(10, solid, WX)]
    h_mf = [Halo(11, mf.at[0], 1, None, False), Halo(12, mf.at[1], 1, None, False)]

    start(h_vel[0] + h_p[0])
    for d in range(3):
        v1[d, own_x, own_y, :] = vel_ref[d]
    pin1[own_x, own_y, :] = p_ref[...]

    column_of = lax.broadcasted_iota(jnp.int32, (columns, slots), 0).astype(F32)
    depth_of = lax.broadcasted_iota(jnp.int32, (nz, slots), 0).astype(F32)
    dep[...] = jnp.zeros_like(dep)
    for k in range(1, n_gy):
        incoming(k).wait_recv()

    def deposit(b, carry):
        hot_c = rk[b, 0:1, :] == column_of
        hot_z = jnp.where(rk[b, 1:2, :] == depth_of, 1.0, 0.0).astype(BF16)
        volume = rk[b, 2:3, :]
        values = [volume] + [volume * rk[b, 3 + d:4 + d, :] for d in range(3)]
        parts = [split(value) for value in values]
        both = None
        for side in (0, 1):
            left = jnp.concatenate([jnp.where(hot_c, part[side], 0.0).astype(BF16) for part in parts], axis=0)
            term = lax.dot_general(left, hot_z, (((1,), (1,)), ((), ())), preferred_element_type=F32)
            both = term if both is None else both + term
        dep[...] += both
        return carry

    lax.fori_loop(0, n_gy, deposit, 0)
    solid[own_x, own_y, :] = dep[pl.ds(0, columns), :].reshape(bx, by, nz)
    for d in range(3):
        mf[d, own_x, own_y, :] = dep[pl.ds((1 + d) * columns, columns), :].reshape(bx, by, nz)
    start(h_solid + h_mf)
    relay(h_vel[0])
    relay(h_p[0])
    relay(h_solid + h_mf)
    arrive(h_solid + h_mf)
    arrive(h_vel[0])

    row = lax.broadcasted_iota(jnp.int32, (ey, nz), 0)
    depth = lax.broadcasted_iota(jnp.int32, (ey, nz), 1)
    row_in = jnp.where((row >= WY) | (iy > 0), 1.0, 0.0) * jnp.where((row < WY + by) | (iy < n_gy - 1), 1.0, 0.0)

    def voidage(x, carry):
        x_in = ((x >= WX) | (ix > 0)) & ((x < WX + bx) | (ix < n_gx - 1))
        eps[x] = jnp.maximum(1.0 - solid[x], FLOOR) * (row_in * jnp.where(x_in, 1.0, 0.0))
        return carry

    lax.fori_loop(0, ex, voidage, 0)

    def up_y(v):
        return pltpu.roll(v, ey - 1, 0)

    def down_y(v):
        return pltpu.roll(v, 1, 0)

    def up_z(v):
        return pltpu.roll(v, nz - 1, 1)

    def down_z(v):
        return pltpu.roll(v, 1, 1)

    last_z, first_z = depth == nz - 1, depth == 0

    def weights(x, carry):
        e = eps[x]
        near = [eps[x + 1], eps[x - 1], up_y(e), down_y(e),
                jnp.where(last_z, 0.0, up_z(e)), jnp.where(first_z, 0.0, down_z(e))]
        total = 0.5 * (6.0 * e + (((near[0] + near[1]) + (near[2] + near[3])) + (near[4] + near[5])))
        inside = e > 0.0
        inverse = jnp.where(inside, 0.5 / jnp.where(inside, total, 1.0), 0.0)
        for n in range(6):
            w = (e + near[n]) * inverse
            if n == 4:
                w = jnp.where(last_z, 0.0, w)
            if n == 5:
                w = jnp.where(first_z, 0.0, w)
            coef[n, x] = w
        coef[6, x] = 2.0 * inverse
        recip = 1.0 / jnp.where(inside, e, 1.0)
        rate[x] = (DT * VISC) * total * recip
        pull[x] = (DT * DRAG) * recip
        return carry

    lax.fori_loop(1, ex - 1, weights, 0)

    def stencil(field, x):
        v = field[x]
        return v, (((coef[0, x] * field[x + 1] + coef[1, x] * field[x - 1])
                    + (coef[2, x] * up_y(v) + coef[3, x] * down_y(v)))
                   + (coef[4, x] * up_z(v) + coef[5, x] * down_z(v)))

    for step in range(STEPS):
        v = (v1, v2)[step]
        pin = (pin1, pin2)[step]
        src = (src1, src2)[step]

        def predict(x, carry):
            s, r, g, e = solid[x], rate[x], pull[x], eps[x]
            for d in range(3):
                old, mean = stencil(v.at[d], x)
                new = old + r * (mean - old) + g * (mf[d, x] - s * old)
                guess[d, x] = new
                flux[d, x] = e * new
            return carry

        lax.fori_loop(WX - 1, WX + bx + 1, predict, 0)

        def balance(x, carry):
            f1, f2 = flux[1, x], flux[2, x]
            out = ((flux[0, x + 1] - flux[0, x - 1]) + (up_y(f1) - down_y(f1))
                   + (jnp.where(last_z, 0.0, up_z(f2)) - jnp.where(first_z, 0.0, down_z(f2))))
            src[x, own_y, :] = (0.5 / DT) * out[WY:WY + by]
            return carry

        lax.fori_loop(WX, WX + bx, balance, 0)
        start(h_src[step])
        if step > 0:
            relay(h_p[step])
        relay(h_src[step])
        arrive(h_p[step])
        arrive(h_src[step])

        def scale(x, carry):
            sp[x] = src[x] * coef[6, x]
            return carry

        lax.fori_loop(1, ex - 1, scale, 0)

        held = pin
        for sweep in range(SWEEPS):
            into = (pa, pb)[sweep % 2]

            def relax(x, carry):
                _, mean = stencil(held, x)
                into[x] = mean - sp[x]
                return carry

            lax.fori_loop(1 + sweep, ex - 1 - sweep, relax, 0)
            held = into

        final = step == STEPS - 1

        def correct(x, carry):
            p = held[x]
            slopes = [held[x + 1] - held[x - 1], up_y(p) - down_y(p),
                      jnp.where(last_z, 0.0, up_z(p)) - jnp.where(first_z, 0.0, down_z(p))]
            for d in range(3):
                new = (guess[d, x] - (0.5 * DT) * slopes[d])[WY:WY + by]
                if final:
                    vel_out[d, x - WX] = new
                else:
                    v2[d, x, own_y, :] = new
            if final:
                p_out[x - WX] = p[WY:WY + by]
            else:
                pin2[x, own_y, :] = p[WY:WY + by]
            return carry

        lax.fori_loop(WX, WX + bx, correct, 0)
        if not final:
            start(h_vel[step + 1])
            start(h_p[step + 1])
            relay(h_vel[step + 1])
            arrive(h_vel[step + 1])

    for f in range(4):
        grid = (vel_out[f] if f < 3 else eps[own_x, own_y, :]).reshape(columns, nz)
        high, low = split(grid.T)
        ft[pl.ds(f * nz, nz), :] = jnp.concatenate([high.astype(BF16), low.astype(BF16)], axis=1)

    def gather(b, carry):
        hot = jnp.where(rk[b, 0:1, :] == column_of, 1.0, 0.0).astype(BF16)
        hot_z = rk[b, 1:2, :] == depth_of
        wide = jnp.dot(ft[...], jnp.concatenate([hot, hot], axis=0), preferred_element_type=F32)
        at = [jnp.sum(jnp.where(hot_z, wide[f * nz:(f + 1) * nz], 0.0), axis=0, keepdims=True) for f in range(4)]
        scaled = rk[b, 2:3, :] * DRAG
        for d in range(3):
            dk[b, d:d + 1, :] = scaled * (at[d] - rk[b, 3 + d:4 + d, :]) / at[3]
        return carry

    lax.fori_loop(0, n_gy, gather, 0)

    def giving(k):
        return particles(k, dk.at[lax.rem(iy + k, n_gy)], rd.at[iy], 1)

    def getting(k):
        return particles(k, dk.at[0], rd.at[lax.rem(iy + n_gy - k, n_gy)], 1)

    for k in range(1, n_gy):
        giving(k).start()
    rd[iy] = dk[iy]
    for h in sent:
        h.each("x", lambda c: c.wait_send())
        h.each("y", lambda c: c.wait_send())
        if h.corners:
            h.each_corner(lambda c: c.wait_send())
    for k in range(1, n_gy):
        outgoing(k).wait_send()
        getting(k).wait_recv()
        giving(k).wait_send()
    for c in range(n_gy):
        drag_out[c] = rd[c, 0:3, :]


def solution(mesh):
    n_gx, n_gy = mesh.shape["gx"], mesh.shape["gy"]

    def per_device(velocity, pressure, part_cell, part_count, grain_velocities, part_vol):
        bx, by, nz = pressure.shape
        slots = part_vol.shape[-1]
        ext = (bx + 2 * WX, by + 2 * WY, nz)
        vmem = pl.BlockSpec(memory_space=pltpu.VMEM)

        def field(*lead):
            return pltpu.VMEM(lead + ext, F32)

        def kernel(*refs):
            body(n_gx, n_gy, *refs)

        v, p, drag = pl.pallas_call(
            kernel,
            name="interval",
            out_shape=(
                jax.ShapeDtypeStruct(velocity.shape, F32),
                jax.ShapeDtypeStruct(pressure.shape, F32),
                jax.ShapeDtypeStruct((n_gy, 3, slots), F32),
            ),
            in_specs=[pl.BlockSpec(memory_space=pltpu.SMEM)] + [vmem] * 5,
            out_specs=(vmem,) * 3,
            scratch_shapes=[
                field(3), field(3), field(), field(), field(), field(), field(), field(), field(),
                field(), field(3), field(), field(7), field(), field(), field(3), field(3),
                pltpu.VMEM((4 * bx * by, nz), F32),
                pltpu.VMEM((n_gy, ROWS, slots), F32),
                pltpu.VMEM((n_gy, ROWS, slots), F32),
                pltpu.VMEM((n_gy, 3, slots), F32),
                pltpu.VMEM((n_gy, 3, slots), F32),
                pltpu.VMEM((4 * nz, 2 * bx * by), BF16),
                pltpu.SemaphoreType.DMA((13, 8)),
                pltpu.SemaphoreType.DMA((13, 8)),
                pltpu.SemaphoreType.DMA((2, n_gy)),
                pltpu.SemaphoreType.DMA((2, n_gy)),
            ],
            compiler_params=pltpu.CompilerParams(
                collective_id=0, has_side_effects=True, vmem_limit_bytes=56 * 1024 * 1024
            ),
        )(
            part_count.reshape(n_gy),
            velocity,
            pressure,
            part_cell.reshape(n_gy, slots),
            grain_velocities.reshape(n_gy, 3, slots),
            part_vol.reshape(n_gy, slots),
        )
        return v, p, drag.reshape(grain_velocities.shape)

    placed = (
        P(None, "gx", "gy", None),
        P("gx", "gy", None),
        P("gx", "gy", None, None),
        P("gx", "gy", None),
        P("gx", "gy", None, None, None),
        P("gx", "gy", None, None),
    )
    return jax.shard_map(
        per_device,
        mesh=mesh,
        in_specs=placed,
        out_specs=(P(None, "gx", "gy", None), P("gx", "gy", None), P("gx", "gy", None, None, None)),
        check_vma=False,
    )
```

```python
import jax
import jax.numpy as jnp
from jax import lax
from jax.experimental import pallas as pl
from jax.experimental.pallas import tpu as pltpu
from jax.sharding import PartitionSpec as P

STEPS = 2
SWEEPS = 4
DRAG = 2.0
DT = 0.25
VISC = 0.2
FLOOR = 0.4

WX = SWEEPS + 1
WY = 8
ROWS = 8

MESH = pl.DeviceIdType.MESH
CORNERS = ((0, 0), (0, 1), (1, 0), (1, 1))
F32 = jnp.float32
BF16 = jnp.bfloat16


def split(value):
    high = value.astype(BF16).astype(F32)
    return high, value - high


def body(n_gx, n_gy, count_ref, vel_ref, p_ref, cell_ref, gv_ref, vol_ref,
         vel_out, p_out, drag_out,
         v1, v2, pin1, pin2, pa, pb, src1, src2, sp, solid, mf, eps, coef, rate, pull,
         guess, flux, dep, pk, rk, dk, rd, ft, corner_out, corner_in, field_send, field_recv, part_send, part_recv):
    bx, by, nz = p_ref.shape
    ex, ey = bx + 2 * WX, by + 2 * WY
    slots = vol_ref.shape[-1]
    columns = bx * by
    ix, iy = lax.axis_index("gx"), lax.axis_index("gy")
    has = {("x", 0): ix > 0, ("x", 1): ix < n_gx - 1, ("y", 0): iy > 0, ("y", 1): iy < n_gy - 1}
    peer = {("x", 0): (ix - 1, iy), ("x", 1): (ix + 1, iy), ("y", 0): (ix, iy - 1), ("y", 1): (ix, iy + 1)}
    own_x, own_y = pl.ds(WX, bx), pl.ds(WY, by)

    def beyond(corner):
        return ix + (2 * corner[0] - 1), iy + (2 * corner[1] - 1)

    barrier = pltpu.get_barrier_semaphore()
    for k in range(1, n_gy):
        pl.semaphore_signal(barrier, inc=1, device_id=(ix, lax.rem(iy + k, n_gy)), device_id_type=MESH)
    for side in (0, 1):
        @pl.when(has["x", side])
        def _():
            pl.semaphore_signal(barrier, inc=1, device_id=peer["x", side], device_id_type=MESH)
    for corner in CORNERS:
        @pl.when(has["x", corner[0]] & has["y", corner[1]])
        def _():
            pl.semaphore_signal(barrier, inc=1, device_id=beyond(corner), device_id_type=MESH)

    slot = lax.broadcasted_iota(jnp.int32, (1, slots), 1)
    for c in range(n_gy):
        cell = cell_ref[pl.ds(c, 1), :]
        column = lax.div(cell, nz)
        pk[c, 0:1, :] = column.astype(F32)
        pk[c, 1:2, :] = (cell - column * nz).astype(F32)
        pk[c, 2:3, :] = jnp.where(slot < count_ref[c], vol_ref[pl.ds(c, 1), :], 0.0)
        for d in range(3):
            pk[c, 3 + d:4 + d, :] = gv_ref[d, pl.ds(c, 1), :]
        pk[c, 6:8, :] = jnp.zeros((2, slots), F32)

    fields = [v1.at[d] for d in range(3)] + [v2.at[d] for d in range(3)] + [mf.at[d] for d in range(3)]
    fields += [pin1, pin2, src1, src2, solid]
    for side in (0, 1):
        @pl.when(jnp.logical_not(has["x", side]))
        def _():
            for field in fields:
                at = 0 if side == 0 else WX + bx
                field[pl.ds(at, WX)] = jnp.zeros((WX, ey, nz), F32)

        @pl.when(jnp.logical_not(has["y", side]))
        def _():
            for field in fields:
                at = 0 if side == 0 else WY + by
                field[:, pl.ds(at, WY), :] = jnp.zeros((ex, WY, nz), F32)

    x_peers = jnp.where(ix > 0, 1, 0) + jnp.where(ix < n_gx - 1, 1, 0)
    y_peers = jnp.where(iy > 0, 1, 0) + jnp.where(iy < n_gy - 1, 1, 0)
    pl.semaphore_wait(barrier, n_gy - 1 + x_peers * (1 + y_peers))

    def particles(k, source, landing, bank):
        return pltpu.make_async_remote_copy(
            src_ref=source, dst_ref=landing, send_sem=part_send.at[bank, k], recv_sem=part_recv.at[bank, k],
            device_id=(ix, lax.rem(iy + k, n_gy)), device_id_type=MESH)

    def outgoing(k):
        return particles(k, pk.at[lax.rem(iy + k, n_gy)], rk.at[iy], 0)

    def incoming(k):
        return particles(k, pk.at[0], rk.at[lax.rem(iy + n_gy - k, n_gy)], 0)

    for k in range(1, n_gy):
        outgoing(k).start()
    rk[iy] = pk[iy]

    class Halo:
        def __init__(self, slot, ref, width, reach=0, own=None, axes="xy", skip=0):
            self.slot, self.ref, self.width, self.own, self.axes, self.skip = slot, ref, width, own, axes, skip
            self.rows = [(i, j) for i in range(reach) for j in range(reach) if i + j + 2 <= reach]

        def copy(self, index, source, landing, to):
            return pltpu.make_async_remote_copy(
                src_ref=source, dst_ref=landing, send_sem=field_send.at[self.slot, index],
                recv_sem=field_recv.at[self.slot, index], device_id=to, device_id_type=MESH)

        def x_copy(self, side):
            w, skip = self.width, self.skip
            at = skip if side == 0 else bx - w - skip
            if self.own is None:
                source = self.ref.at[pl.ds(WX + at, w), own_y]
            else:
                source = self.own.at[pl.ds(at, w)]
            landing = self.ref.at[pl.ds(WX + bx + skip if side == 0 else WX - w - skip, w), own_y]
            return self.copy(side, source, landing, peer["x", side])

        def y_copy(self, side):
            at = 0 if side == 0 else by - WY
            if self.own is None:
                source = self.ref.at[own_x, pl.ds(WY + at, WY)]
            else:
                source = self.own.at[:, pl.ds(at, WY)]
            landing = self.ref.at[own_x, pl.ds(WY + by if side == 0 else 0, WY)]
            return self.copy(2 + side, source, landing, peer["y", side])

        def c_copy(self, corner):
            n = 2 * corner[0] + corner[1]
            size = -(-len(self.rows) // 8) * 8
            return self.copy(4 + n, corner_out.at[self.slot, n, pl.ds(0, size)],
                             corner_in.at[self.slot, n, pl.ds(0, size)], beyond(corner))

        def pack(self):
            for corner in CORNERS if self.rows else ():
                for n, (i, j) in enumerate(self.rows):
                    x = WX + (i if corner[0] == 0 else bx - 1 - i)
                    y = WY + (j if corner[1] == 0 else by - 1 - j)
                    corner_out[self.slot, 2 * corner[0] + corner[1], n:n + 1, :] = self.ref[x, y:y + 1, :]

        def each(self, axis, act, flip=False):
            if axis == "c":
                for corner in CORNERS if self.rows else ():
                    near = (1 - corner[0], 1 - corner[1]) if flip else corner

                    @pl.when(has["x", near[0]] & has["y", near[1]])
                    def _():
                        act(self.c_copy(corner), corner)
            elif axis in self.axes:
                for side in (0, 1):
                    @pl.when(has[axis, 1 - side if flip else side])
                    def _():
                        act((self.x_copy if axis == "x" else self.y_copy)(side), None)

        def unpack(self, copy, corner):
            copy.wait_recv()
            for n, (i, j) in enumerate(self.rows):
                x = WX + bx + i if corner[0] == 0 else WX - 1 - i
                y = WY + by + j if corner[1] == 0 else WY - 1 - j
                self.ref[x, y:y + 1, :] = corner_in[self.slot, 2 * corner[0] + corner[1], n:n + 1, :]

    sent = []

    def start(halos):
        for h in halos:
            h.pack()
        for axis in "xcy":
            for h in halos:
                h.each(axis, lambda c, _: c.start())
        sent.extend(halos)

    def arrive(halos):
        for h in halos:
            h.each("y", lambda c, _: c.wait_recv(), flip=True)
            h.each("x", lambda c, _: c.wait_recv(), flip=True)
        for h in halos:
            h.each("c", h.unpack, flip=True)

    h_vel = [[Halo(0, v1.at[0], 2, 2, vel_ref.at[0]), Halo(1, v1.at[1], 1, 2, vel_ref.at[1]), Halo(2, v1.at[2], 1, 0, vel_ref.at[2])],
             [Halo(3, v2.at[0], 2, 2), Halo(4, v2.at[1], 1, 2), Halo(5, v2.at[2], 1)]]
    h_p = [[Halo(6, pin1, WX, WX, p_ref)], [Halo(7, pin2, WX, WX)]]
    h_src = [[Halo(8, src1, SWEEPS, SWEEPS)], [Halo(9, src2, SWEEPS, SWEEPS)]]
    h_solid = [Halo(10, solid, 2, WX)]
    h_rest = [Halo(13, solid, WX - 2, axes="x", skip=2)]
    h_mf = [Halo(11, mf.at[0], 1, axes="x"), Halo(12, mf.at[1], 1, axes="y")]

    for d in range(3):
        v1[d, own_x, own_y, :] = vel_ref[d]
    pin1[own_x, own_y, :] = p_ref[...]
    start(h_vel[0] + h_p[0])

    column_of = lax.broadcasted_iota(jnp.int32, (columns, slots), 0).astype(F32)
    depth_of = lax.broadcasted_iota(jnp.int32, (nz, slots), 0).astype(F32)
    dep[...] = jnp.zeros_like(dep)
    def deposit(b, carry):
        hot_c = rk[b, 0:1, :] == column_of
        hot_z = jnp.where(rk[b, 1:2, :] == depth_of, 1.0, 0.0).astype(BF16)
        volume = rk[b, 2:3, :]
        values = [volume] + [volume * rk[b, 3 + d:4 + d, :] for d in range(3)]
        parts = [split(value) for value in values]
        both = None
        for side in (0, 1):
            left = jnp.concatenate([jnp.where(hot_c, part[side], 0.0).astype(BF16) for part in parts], axis=0)
            term = lax.dot_general(left, hot_z, (((1,), (1,)), ((), ())), preferred_element_type=F32)
            both = term if both is None else both + term
        dep[...] += both
        return carry

    deposit(iy, 0)

    def deposit_from(k, carry):
        incoming(k).wait_recv()
        return deposit(lax.rem(iy + n_gy - k, n_gy), carry)

    lax.fori_loop(1, n_gy, deposit_from, 0)
    solid[own_x, own_y, :] = dep[pl.ds(0, columns), :].reshape(bx, by, nz)
    for d in range(3):
        mf[d, own_x, own_y, :] = dep[pl.ds((1 + d) * columns, columns), :].reshape(bx, by, nz)
    start(h_solid + h_mf)
    start(h_rest)
    arrive(h_solid + h_mf)
    arrive(h_vel[0])

    row = lax.broadcasted_iota(jnp.int32, (ey, nz), 0)
    depth = lax.broadcasted_iota(jnp.int32, (ey, nz), 1)
    row_in = jnp.where((row >= WY) | (iy > 0), 1.0, 0.0) * jnp.where((row < WY + by) | (iy < n_gy - 1), 1.0, 0.0)

    def voidage(x, carry):
        x_in = ((x >= WX) | (ix > 0)) & ((x < WX + bx) | (ix < n_gx - 1))
        eps[x] = jnp.maximum(1.0 - solid[x], FLOOR) * (row_in * jnp.where(x_in, 1.0, 0.0))
        return carry

    lax.fori_loop(WX - 2, WX + bx + 2, voidage, 0, unroll=4)

    def up_y(v):
        return pltpu.roll(v, ey - 1, 0)

    def down_y(v):
        return pltpu.roll(v, 1, 0)

    def up_z(v):
        return pltpu.roll(v, nz - 1, 1)

    def down_z(v):
        return pltpu.roll(v, 1, 1)

    last_z, first_z = depth == nz - 1, depth == 0

    def weights(x, carry):
        e = eps[x]
        near = [eps[x + 1], eps[x - 1], up_y(e), down_y(e),
                jnp.where(last_z, 0.0, up_z(e)), jnp.where(first_z, 0.0, down_z(e))]
        total = 0.5 * (6.0 * e + (((near[0] + near[1]) + (near[2] + near[3])) + (near[4] + near[5])))
        inside = e > 0.0
        inverse = jnp.where(inside, 0.5 / jnp.where(inside, total, 1.0), 0.0)
        for n in range(6):
            w = (e + near[n]) * inverse
            if n == 4:
                w = jnp.where(last_z, 0.0, w)
            if n == 5:
                w = jnp.where(first_z, 0.0, w)
            coef[n, x] = w
        coef[6, x] = 2.0 * inverse
        recip = 1.0 / jnp.where(inside, e, 1.0)
        rate[x] = (DT * VISC) * total * recip
        pull[x] = (DT * DRAG) * recip
        return carry

    lax.fori_loop(WX - 1, WX + bx + 1, weights, 0, unroll=5)

    def stencil(field, x):
        v = field[x]
        return v, (((coef[0, x] * field[x + 1] + coef[1, x] * field[x - 1])
                    + (coef[2, x] * up_y(v) + coef[3, x] * down_y(v)))
                   + (coef[4, x] * up_z(v) + coef[5, x] * down_z(v)))

    for step in range(STEPS):
        v = (v1, v2)[step]
        pin = (pin1, pin2)[step]
        src = (src1, src2)[step]

        def predict(x, carry):
            s, r, g, e = solid[x], rate[x], pull[x], eps[x]
            for d in range(3):
                old, mean = stencil(v.at[d], x)
                new = old + r * (mean - old) + g * (mf[d, x] - s * old)
                guess[d, x] = new
                flux[d, x] = e * new
            return carry

        lax.fori_loop(WX - 1, WX + bx + 1, predict, 0, unroll=5)

        def balance(x, carry):
            f1, f2 = flux[1, x], flux[2, x]
            out = ((flux[0, x + 1] - flux[0, x - 1]) + (up_y(f1) - down_y(f1))
                   + (jnp.where(last_z, 0.0, up_z(f2)) - jnp.where(first_z, 0.0, down_z(f2))))
            src[x, own_y, :] = (0.5 / DT) * out[WY:WY + by]
            return carry

        lax.fori_loop(WX, WX + bx, balance, 0, unroll=8)
        start(h_src[step])
        if step == 0:
            arrive(h_rest)
            for low in (0, WX + bx + 2):
                lax.fori_loop(low, low + WX - 2, voidage, 0, unroll=3)
            for low in (1, WX + bx + 1):
                lax.fori_loop(low, low + WX - 2, weights, 0, unroll=3)
        arrive(h_p[step])
        arrive(h_src[step])

        def scale(x, carry):
            sp[x] = src[x] * coef[6, x]
            return carry

        lax.fori_loop(1, ex - 1, scale, 0, unroll=8)

        held = pin
        for sweep in range(SWEEPS):
            into = (pa, pb)[sweep % 2]

            def relax(x, carry):
                _, mean = stencil(held, x)
                into[x] = mean - sp[x]
                return carry

            lax.fori_loop(1 + sweep, ex - 1 - sweep, relax, 0, unroll=4)
            held = into

        final = step == STEPS - 1

        def correct(x, carry):
            p = held[x]
            slopes = [held[x + 1] - held[x - 1], up_y(p) - down_y(p),
                      jnp.where(last_z, 0.0, up_z(p)) - jnp.where(first_z, 0.0, down_z(p))]
            for d in range(3):
                new = (guess[d, x] - (0.5 * DT) * slopes[d])[WY:WY + by]
                if final:
                    vel_out[d, x - WX] = new
                else:
                    v2[d, x, own_y, :] = new
            if final:
                p_out[x - WX] = p[WY:WY + by]
            else:
                pin2[x, own_y, :] = p[WY:WY + by]
            return carry

        lax.fori_loop(WX, WX + bx, correct, 0, unroll=4)
        if not final:
            start(h_vel[step + 1])
            start(h_p[step + 1])
            arrive(h_vel[step + 1])

    for f in range(4):
        grid = (vel_out[f] if f < 3 else eps[own_x, own_y, :]).reshape(columns, nz)
        high, low = split(grid.T)
        ft[pl.ds(f * nz, nz), :] = jnp.concatenate([high.astype(BF16), low.astype(BF16)], axis=1)

    def gather(b, carry):
        hot = jnp.where(rk[b, 0:1, :] == column_of, 1.0, 0.0).astype(BF16)
        hot_z = rk[b, 1:2, :] == depth_of
        wide = jnp.dot(ft[...], jnp.concatenate([hot, hot], axis=0), preferred_element_type=F32)
        at = [jnp.sum(jnp.where(hot_z, wide[f * nz:(f + 1) * nz], 0.0), axis=0, keepdims=True) for f in range(4)]
        scaled = rk[b, 2:3, :] * DRAG
        for d in range(3):
            dk[b, d:d + 1, :] = scaled * (at[d] - rk[b, 3 + d:4 + d, :]) / at[3]
        return carry

    def giving(k):
        return particles(k, dk.at[lax.rem(iy + k, n_gy)], rd.at[iy], 1)

    def getting(k):
        return particles(k, dk.at[0], rd.at[lax.rem(iy + n_gy - k, n_gy)], 1)

    def gather_for(k, carry):
        gather(lax.rem(iy + k, n_gy), carry)
        giving(k).start()
        return carry

    lax.fori_loop(1, n_gy, gather_for, 0)
    gather(iy, 0)
    rd[iy] = dk[iy]
    for h in sent:
        for axis in "xyc":
            h.each(axis, lambda c, _: c.wait_send())
    for k in range(1, n_gy):
        outgoing(k).wait_send()
        getting(k).wait_recv()
        giving(k).wait_send()
    for c in range(n_gy):
        for d in range(3):
            drag_out[d, pl.ds(c, 1), :] = rd[c, d:d + 1, :]


def solution(mesh):
    n_gx, n_gy = mesh.shape["gx"], mesh.shape["gy"]

    def per_device(velocity, pressure, part_cell, part_count, grain_velocities, part_vol):
        bx, by, nz = pressure.shape
        slots = part_vol.shape[-1]
        ext = (bx + 2 * WX, by + 2 * WY, nz)
        vmem = pl.BlockSpec(memory_space=pltpu.VMEM)

        def field(*lead):
            return pltpu.VMEM(lead + ext, F32)

        def kernel(*refs):
            body(n_gx, n_gy, *refs)

        v, p, drag = pl.pallas_call(
            kernel,
            name="interval",
            out_shape=(
                jax.ShapeDtypeStruct(velocity.shape, F32),
                jax.ShapeDtypeStruct(pressure.shape, F32),
                jax.ShapeDtypeStruct((3, n_gy, slots), F32),
            ),
            in_specs=[pl.BlockSpec(memory_space=pltpu.SMEM)] + [vmem] * 5,
            out_specs=(vmem,) * 3,
            scratch_shapes=[
                field(3), field(3), field(), field(), field(), field(), field(), field(), field(),
                field(), field(3), field(), field(7), field(), field(), field(3), field(3),
                pltpu.VMEM((4 * bx * by, nz), F32),
                pltpu.VMEM((n_gy, ROWS, slots), F32),
                pltpu.VMEM((n_gy, ROWS, slots), F32),
                pltpu.VMEM((n_gy, 3, slots), F32),
                pltpu.VMEM((n_gy, 3, slots), F32),
                pltpu.VMEM((4 * nz, 2 * bx * by), BF16),
                pltpu.VMEM((14, 4, 16, nz), F32),
                pltpu.VMEM((14, 4, 16, nz), F32),
                pltpu.SemaphoreType.DMA((14, 8)),
                pltpu.SemaphoreType.DMA((14, 8)),
                pltpu.SemaphoreType.DMA((2, n_gy)),
                pltpu.SemaphoreType.DMA((2, n_gy)),
            ],
            compiler_params=pltpu.CompilerParams(
                collective_id=0, has_side_effects=True, vmem_limit_bytes=56 * 1024 * 1024
            ),
        )(
            part_count.reshape(n_gy),
            velocity,
            pressure,
            part_cell.reshape(n_gy, slots),
            grain_velocities.reshape(n_gy, 3, slots).transpose(1, 0, 2),
            part_vol.reshape(n_gy, slots),
        )
        return v, p, drag.transpose(1, 0, 2).reshape(grain_velocities.shape)

    placed = (
        P(None, "gx", "gy", None),
        P("gx", "gy", None),
        P("gx", "gy", None, None),
        P("gx", "gy", None),
        P("gx", "gy", None, None, None),
        P("gx", "gy", None, None),
    )
    return jax.shard_map(
        per_device,
        mesh=mesh,
        in_specs=placed,
        out_specs=(P(None, "gx", "gy", None), P("gx", "gy", None), P("gx", "gy", None, None, None)),
        check_vma=False,
    )
```

```python
import jax
import jax.numpy as jnp
from jax import lax
from jax.experimental import pallas as pl
from jax.experimental.pallas import tpu as pltpu
from jax.sharding import PartitionSpec as P

STEPS = 2
SWEEPS = 4
DRAG = 2.0
DT = 0.25
VISC = 0.2
FLOOR = 0.4

WX = SWEEPS + 1
WY = 8
ROWS = 8

MESH = pl.DeviceIdType.MESH
CORNERS = ((0, 0), (0, 1), (1, 0), (1, 1))
F32 = jnp.float32
BF16 = jnp.bfloat16


def split(value):
    high = value.astype(BF16).astype(F32)
    return high, value - high


def body(n_gx, n_gy, count_ref, vel_ref, p_ref, cell_ref, gv_ref, vol_ref,
         vel_out, p_out, drag_out,
         v1, v2, pin1, pin2, pa, pb, src1, src2, sp, solid, mf, eps, coef, rate, pull,
         guess, flux, dep, pk, rk, dk, rd, ft, corner_out, corner_in, field_send, field_recv, part_send, part_recv):
    bx, by, nz = p_ref.shape
    ex, ey = bx + 2 * WX, by + 2 * WY
    slots = vol_ref.shape[-1]
    columns = bx * by
    ix, iy = lax.axis_index("gx"), lax.axis_index("gy")
    has = {("x", 0): ix > 0, ("x", 1): ix < n_gx - 1, ("y", 0): iy > 0, ("y", 1): iy < n_gy - 1}
    peer = {("x", 0): (ix - 1, iy), ("x", 1): (ix + 1, iy), ("y", 0): (ix, iy - 1), ("y", 1): (ix, iy + 1)}
    own_x, own_y = pl.ds(WX, bx), pl.ds(WY, by)

    def beyond(corner):
        return ix + (2 * corner[0] - 1), iy + (2 * corner[1] - 1)

    barrier = pltpu.get_barrier_semaphore()
    for k in range(1, n_gy):
        pl.semaphore_signal(barrier, inc=1, device_id=(ix, lax.rem(iy + k, n_gy)), device_id_type=MESH)
    for side in (0, 1):
        @pl.when(has["x", side])
        def _():
            pl.semaphore_signal(barrier, inc=1, device_id=peer["x", side], device_id_type=MESH)
    for corner in CORNERS:
        @pl.when(has["x", corner[0]] & has["y", corner[1]])
        def _():
            pl.semaphore_signal(barrier, inc=1, device_id=beyond(corner), device_id_type=MESH)

    slot = lax.broadcasted_iota(jnp.int32, (1, slots), 1)
    for c in range(n_gy):
        cell = cell_ref[pl.ds(c, 1), :]
        column = lax.div(cell, nz)
        pk[c, 0:1, :] = column.astype(F32)
        pk[c, 1:2, :] = (cell - column * nz).astype(F32)
        pk[c, 2:3, :] = jnp.where(slot < count_ref[c], vol_ref[pl.ds(c, 1), :], 0.0)
        for d in range(3):
            pk[c, 3 + d:4 + d, :] = gv_ref[d, pl.ds(c, 1), :]
        pk[c, 6:8, :] = jnp.zeros((2, slots), F32)

    fields = [v1.at[d] for d in range(3)] + [v2.at[d] for d in range(3)] + [mf.at[d] for d in range(3)]
    fields += [pin1, pin2, src1, src2, solid]
    for side in (0, 1):
        @pl.when(jnp.logical_not(has["x", side]))
        def _():
            for field in fields:
                at = 0 if side == 0 else WX + bx
                field[pl.ds(at, WX)] = jnp.zeros((WX, ey, nz), F32)

        @pl.when(jnp.logical_not(has["y", side]))
        def _():
            for field in fields:
                at = 0 if side == 0 else WY + by
                field[:, pl.ds(at, WY), :] = jnp.zeros((ex, WY, nz), F32)

    x_peers = jnp.where(ix > 0, 1, 0) + jnp.where(ix < n_gx - 1, 1, 0)
    y_peers = jnp.where(iy > 0, 1, 0) + jnp.where(iy < n_gy - 1, 1, 0)
    pl.semaphore_wait(barrier, n_gy - 1 + x_peers * (1 + y_peers))

    def particles(k, source, landing, bank):
        return pltpu.make_async_remote_copy(
            src_ref=source, dst_ref=landing, send_sem=part_send.at[bank, k], recv_sem=part_recv.at[bank, k],
            device_id=(ix, lax.rem(iy + k, n_gy)), device_id_type=MESH)

    def outgoing(k):
        return particles(k, pk.at[lax.rem(iy + k, n_gy)], rk.at[iy], 0)

    def incoming(k):
        return particles(k, pk.at[0], rk.at[lax.rem(iy + n_gy - k, n_gy)], 0)

    for k in range(1, n_gy):
        outgoing(k).start()
    rk[iy] = pk[iy]

    class Halo:
        def __init__(self, slot, ref, width, reach=0, own=None, axes="xy", skip=0):
            self.slot, self.ref, self.width, self.own, self.axes, self.skip = slot, ref, width, own, axes, skip
            self.rows = [(i, j) for i in range(reach) for j in range(reach) if i + j + 2 <= reach]

        def copy(self, index, source, landing, to):
            return pltpu.make_async_remote_copy(
                src_ref=source, dst_ref=landing, send_sem=field_send.at[self.slot, index],
                recv_sem=field_recv.at[self.slot, index], device_id=to, device_id_type=MESH)

        def x_copy(self, side):
            w, skip = self.width, self.skip
            at = skip if side == 0 else bx - w - skip
            if self.own is None:
                source = self.ref.at[pl.ds(WX + at, w), own_y]
            else:
                source = self.own.at[pl.ds(at, w)]
            landing = self.ref.at[pl.ds(WX + bx + skip if side == 0 else WX - w - skip, w), own_y]
            return self.copy(side, source, landing, peer["x", side])

        def y_copy(self, side):
            at = 0 if side == 0 else by - WY
            if self.own is None:
                source = self.ref.at[own_x, pl.ds(WY + at, WY)]
            else:
                source = self.own.at[:, pl.ds(at, WY)]
            landing = self.ref.at[own_x, pl.ds(WY + by if side == 0 else 0, WY)]
            return self.copy(2 + side, source, landing, peer["y", side])

        def c_copy(self, corner):
            n = 2 * corner[0] + corner[1]
            size = -(-len(self.rows) // 8) * 8
            return self.copy(4 + n, corner_out.at[self.slot, n, pl.ds(0, size)],
                             corner_in.at[self.slot, n, pl.ds(0, size)], beyond(corner))

        def pack(self):
            for corner in CORNERS if self.rows else ():
                for n, (i, j) in enumerate(self.rows):
                    x = WX + (i if corner[0] == 0 else bx - 1 - i)
                    y = WY + (j if corner[1] == 0 else by - 1 - j)
                    corner_out[self.slot, 2 * corner[0] + corner[1], n:n + 1, :] = self.ref[x, y:y + 1, :]

        def each(self, axis, act, flip=False):
            if axis == "c":
                for corner in CORNERS if self.rows else ():
                    near = (1 - corner[0], 1 - corner[1]) if flip else corner

                    @pl.when(has["x", near[0]] & has["y", near[1]])
                    def _():
                        act(self.c_copy(corner), corner)
            elif axis in self.axes:
                for side in (0, 1):
                    @pl.when(has[axis, 1 - side if flip else side])
                    def _():
                        act((self.x_copy if axis == "x" else self.y_copy)(side), None)

        def unpack(self, copy, corner):
            copy.wait_recv()
            for n, (i, j) in enumerate(self.rows):
                x = WX + bx + i if corner[0] == 0 else WX - 1 - i
                y = WY + by + j if corner[1] == 0 else WY - 1 - j
                self.ref[x, y:y + 1, :] = corner_in[self.slot, 2 * corner[0] + corner[1], n:n + 1, :]

    sent = []

    def start(halos):
        for h in halos:
            h.pack()
        for axis in "cxy":
            for h in halos:
                h.each(axis, lambda c, _: c.start())
        sent.extend(halos)

    def arrive(halos):
        for h in halos:
            h.each("y", lambda c, _: c.wait_recv(), flip=True)
            h.each("x", lambda c, _: c.wait_recv(), flip=True)
        for h in halos:
            h.each("c", h.unpack, flip=True)

    h_vel = [[Halo(0, v1.at[0], 2, 2, vel_ref.at[0]), Halo(1, v1.at[1], 1, 2, vel_ref.at[1]), Halo(2, v1.at[2], 1, 0, vel_ref.at[2])],
             [Halo(3, v2.at[0], 2, 2), Halo(4, v2.at[1], 1, 2), Halo(5, v2.at[2], 1)]]
    h_p = [[Halo(6, pin1, WX, WX, p_ref)], [Halo(7, pin2, WX, WX)]]
    h_src = [[Halo(8, src1, SWEEPS, SWEEPS)], [Halo(9, src2, SWEEPS, SWEEPS)]]
    h_solid = [Halo(10, solid, 2, WX)]
    h_rest = [Halo(13, solid, WX - 2, axes="x", skip=2)]
    h_mf = [Halo(11, mf.at[0], 1, axes="x"), Halo(12, mf.at[1], 1, axes="y")]

    for d in range(3):
        v1[d, own_x, own_y, :] = vel_ref[d]
    pin1[own_x, own_y, :] = p_ref[...]
    start(h_vel[0] + h_p[0])

    column_of = lax.broadcasted_iota(jnp.int32, (columns, slots), 0).astype(F32)
    depth_of = lax.broadcasted_iota(jnp.int32, (nz, slots), 0).astype(F32)
    dep[...] = jnp.zeros_like(dep)
    def deposit(b, carry):
        hot_c = rk[b, 0:1, :] == column_of
        hot_z = jnp.where(rk[b, 1:2, :] == depth_of, 1.0, 0.0).astype(BF16)
        volume = rk[b, 2:3, :]
        values = [volume] + [volume * rk[b, 3 + d:4 + d, :] for d in range(3)]
        parts = [split(value) for value in values]
        both = None
        for side in (0, 1):
            left = jnp.concatenate([jnp.where(hot_c, part[side], 0.0).astype(BF16) for part in parts], axis=0)
            term = lax.dot_general(left, hot_z, (((1,), (1,)), ((), ())), preferred_element_type=F32)
            both = term if both is None else both + term
        dep[...] += both
        return carry

    deposit(iy, 0)

    def deposit_from(k, carry):
        incoming(k).wait_recv()
        return deposit(lax.rem(iy + n_gy - k, n_gy), carry)

    lax.fori_loop(1, n_gy, deposit_from, 0)
    solid[own_x, own_y, :] = dep[pl.ds(0, columns), :].reshape(bx, by, nz)
    for d in range(3):
        mf[d, own_x, own_y, :] = dep[pl.ds((1 + d) * columns, columns), :].reshape(bx, by, nz)
    start(h_solid + h_mf)
    start(h_rest)
    arrive(h_solid + h_mf)
    arrive(h_vel[0])

    row = lax.broadcasted_iota(jnp.int32, (ey, nz), 0)
    depth = lax.broadcasted_iota(jnp.int32, (ey, nz), 1)
    row_in = jnp.where((row >= WY) | (iy > 0), 1.0, 0.0) * jnp.where((row < WY + by) | (iy < n_gy - 1), 1.0, 0.0)

    def voidage(x, carry):
        x_in = ((x >= WX) | (ix > 0)) & ((x < WX + bx) | (ix < n_gx - 1))
        eps[x] = jnp.maximum(1.0 - solid[x], FLOOR) * (row_in * jnp.where(x_in, 1.0, 0.0))
        return carry

    lax.fori_loop(WX - 2, WX + bx + 2, voidage, 0, unroll=4)

    def up_y(v):
        return pltpu.roll(v, ey - 1, 0)

    def down_y(v):
        return pltpu.roll(v, 1, 0)

    def up_z(v):
        return pltpu.roll(v, nz - 1, 1)

    def down_z(v):
        return pltpu.roll(v, 1, 1)

    last_z, first_z = depth == nz - 1, depth == 0

    def weights(x, carry):
        e = eps[x]
        near = [eps[x + 1], eps[x - 1], up_y(e), down_y(e),
                jnp.where(last_z, 0.0, up_z(e)), jnp.where(first_z, 0.0, down_z(e))]
        total = 0.5 * (6.0 * e + (((near[0] + near[1]) + (near[2] + near[3])) + (near[4] + near[5])))
        inside = e > 0.0
        inverse = jnp.where(inside, 0.5 / jnp.where(inside, total, 1.0), 0.0)
        for n in range(6):
            w = (e + near[n]) * inverse
            if n == 4:
                w = jnp.where(last_z, 0.0, w)
            if n == 5:
                w = jnp.where(first_z, 0.0, w)
            coef[n, x] = w
        coef[6, x] = 2.0 * inverse
        recip = 1.0 / jnp.where(inside, e, 1.0)
        rate[x] = (DT * VISC) * total * recip
        pull[x] = (DT * DRAG) * recip
        return carry

    lax.fori_loop(WX - 1, WX + bx + 1, weights, 0, unroll=5)

    def stencil(field, x):
        v = field[x]
        return v, (((coef[0, x] * field[x + 1] + coef[1, x] * field[x - 1])
                    + (coef[2, x] * up_y(v) + coef[3, x] * down_y(v)))
                   + (coef[4, x] * up_z(v) + coef[5, x] * down_z(v)))

    for step in range(STEPS):
        v = (v1, v2)[step]
        pin = (pin1, pin2)[step]
        src = (src1, src2)[step]

        def predict(x, carry):
            s, r, g, e = solid[x], rate[x], pull[x], eps[x]
            for d in range(3):
                old, mean = stencil(v.at[d], x)
                new = old + r * (mean - old) + g * (mf[d, x] - s * old)
                guess[d, x] = new
                flux[d, x] = e * new
            return carry

        lax.fori_loop(WX - 1, WX + bx + 1, predict, 0, unroll=5)

        def balance(x, carry):
            f1, f2 = flux[1, x], flux[2, x]
            out = ((flux[0, x + 1] - flux[0, x - 1]) + (up_y(f1) - down_y(f1))
                   + (jnp.where(last_z, 0.0, up_z(f2)) - jnp.where(first_z, 0.0, down_z(f2))))
            src[x, own_y, :] = (0.5 / DT) * out[WY:WY + by]
            return carry

        lax.fori_loop(WX, WX + bx, balance, 0, unroll=8)
        start(h_src[step])
        if step == 0:
            arrive(h_rest)
            for low in (0, WX + bx + 2):
                lax.fori_loop(low, low + WX - 2, voidage, 0, unroll=3)
            for low in (1, WX + bx + 1):
                lax.fori_loop(low, low + WX - 2, weights, 0, unroll=3)
        arrive(h_p[step])
        arrive(h_src[step])

        def scale(x, carry):
            sp[x] = src[x] * coef[6, x]
            return carry

        lax.fori_loop(1, ex - 1, scale, 0, unroll=8)

        held = pin
        for sweep in range(SWEEPS):
            into = (pa, pb)[sweep % 2]

            def relax(x, carry):
                _, mean = stencil(held, x)
                into[x] = mean - sp[x]
                return carry

            lax.fori_loop(1 + sweep, ex - 1 - sweep, relax, 0, unroll=4)
            held = into

        final = step == STEPS - 1

        def correct(x, carry):
            p = held[x]
            slopes = [held[x + 1] - held[x - 1], up_y(p) - down_y(p),
                      jnp.where(last_z, 0.0, up_z(p)) - jnp.where(first_z, 0.0, down_z(p))]
            for d in range(3):
                new = (guess[d, x] - (0.5 * DT) * slopes[d])[WY:WY + by]
                if final:
                    vel_out[d, x - WX] = new
                else:
                    v2[d, x, own_y, :] = new
            if final:
                p_out[x - WX] = p[WY:WY + by]
            else:
                pin2[x, own_y, :] = p[WY:WY + by]
            return carry

        lax.fori_loop(WX, WX + bx, correct, 0, unroll=4)
        if not final:
            start(h_vel[step + 1])
            start(h_p[step + 1])
            arrive(h_vel[step + 1])

    for f in range(4):
        grid = (vel_out[f] if f < 3 else eps[own_x, own_y, :]).reshape(columns, nz)
        high, low = split(grid.T)
        ft[pl.ds(f * nz, nz), :] = jnp.concatenate([high.astype(BF16), low.astype(BF16)], axis=1)

    def gather(b, carry):
        hot = jnp.where(rk[b, 0:1, :] == column_of, 1.0, 0.0).astype(BF16)
        hot_z = rk[b, 1:2, :] == depth_of
        wide = jnp.dot(ft[...], jnp.concatenate([hot, hot], axis=0), preferred_element_type=F32)
        at = [jnp.sum(jnp.where(hot_z, wide[f * nz:(f + 1) * nz], 0.0), axis=0, keepdims=True) for f in range(4)]
        scaled = rk[b, 2:3, :] * DRAG
        for d in range(3):
            dk[b, d:d + 1, :] = scaled * (at[d] - rk[b, 3 + d:4 + d, :]) / at[3]
        return carry

    def giving(k):
        return particles(k, dk.at[lax.rem(iy + k, n_gy)], rd.at[iy], 1)

    def getting(k):
        return particles(k, dk.at[0], rd.at[lax.rem(iy + n_gy - k, n_gy)], 1)

    def gather_for(k, carry):
        gather(lax.rem(iy + k, n_gy), carry)
        giving(k).start()
        return carry

    lax.fori_loop(1, n_gy, gather_for, 0)
    gather(iy, 0)
    rd[iy] = dk[iy]
    for h in sent:
        for axis in "xyc":
            h.each(axis, lambda c, _: c.wait_send())
    for k in range(1, n_gy):
        outgoing(k).wait_send()
        getting(k).wait_recv()
        giving(k).wait_send()
    for c in range(n_gy):
        for d in range(3):
            drag_out[d, pl.ds(c, 1), :] = rd[c, d:d + 1, :]


def solution(mesh):
    n_gx, n_gy = mesh.shape["gx"], mesh.shape["gy"]

    def per_device(velocity, pressure, part_cell, part_count, grain_velocities, part_vol):
        bx, by, nz = pressure.shape
        slots = part_vol.shape[-1]
        ext = (bx + 2 * WX, by + 2 * WY, nz)
        vmem = pl.BlockSpec(memory_space=pltpu.VMEM)

        def field(*lead):
            return pltpu.VMEM(lead + ext, F32)

        def kernel(*refs):
            body(n_gx, n_gy, *refs)

        v, p, drag = pl.pallas_call(
            kernel,
            name="interval",
            out_shape=(
                jax.ShapeDtypeStruct(velocity.shape, F32),
                jax.ShapeDtypeStruct(pressure.shape, F32),
                jax.ShapeDtypeStruct((3, n_gy, slots), F32),
            ),
            in_specs=[pl.BlockSpec(memory_space=pltpu.SMEM)] + [vmem] * 5,
            out_specs=(vmem,) * 3,
            scratch_shapes=[
                field(3), field(3), field(), field(), field(), field(), field(), field(), field(),
                field(), field(3), field(), field(7), field(), field(), field(3), field(3),
                pltpu.VMEM((4 * bx * by, nz), F32),
                pltpu.VMEM((n_gy, ROWS, slots), F32),
                pltpu.VMEM((n_gy, ROWS, slots), F32),
                pltpu.VMEM((n_gy, 3, slots), F32),
                pltpu.VMEM((n_gy, 3, slots), F32),
                pltpu.VMEM((4 * nz, 2 * bx * by), BF16),
                pltpu.VMEM((14, 4, 16, nz), F32),
                pltpu.VMEM((14, 4, 16, nz), F32),
                pltpu.SemaphoreType.DMA((14, 8)),
                pltpu.SemaphoreType.DMA((14, 8)),
                pltpu.SemaphoreType.DMA((2, n_gy)),
                pltpu.SemaphoreType.DMA((2, n_gy)),
            ],
            compiler_params=pltpu.CompilerParams(
                collective_id=0, has_side_effects=True, vmem_limit_bytes=56 * 1024 * 1024
            ),
        )(
            part_count.reshape(n_gy),
            velocity,
            pressure,
            part_cell.reshape(n_gy, slots),
            grain_velocities.reshape(n_gy, 3, slots).transpose(1, 0, 2),
            part_vol.reshape(n_gy, slots),
        )
        return v, p, drag.transpose(1, 0, 2).reshape(grain_velocities.shape)

    placed = (
        P(None, "gx", "gy", None),
        P("gx", "gy", None),
        P("gx", "gy", None, None),
        P("gx", "gy", None),
        P("gx", "gy", None, None, None),
        P("gx", "gy", None, None),
    )
    return jax.shard_map(
        per_device,
        mesh=mesh,
        in_specs=placed,
        out_specs=(P(None, "gx", "gy", None), P("gx", "gy", None), P("gx", "gy", None, None, None)),
        check_vma=False,
    )
```
